32 devices in a mesh: gx: 8 (over z, core), gy: 4 (over y, x).
Axes of the slice: x: 2, y: 2, z: 4, core: 2. Of those that a mesh axis runs over, the one named last changes fastest.
Arguments:
- diag_blocks: bfloat16 [32, 64, 128, 128], P('gy', 'gx'), may hold values from -0.13 to 4.25
- edge_blocks: bfloat16 [32, 64, 2, 128, 128], P('gy', 'gx'), may hold values from -1.8 to 0.13
- left_pick: int32 [32, 8], P('gy', 'gx'), may hold values from -4 to 4
- right_pick: int32 [32, 8], P('gy', 'gx'), may hold values from -4 to 4
Outputs:
- pivots: bfloat16 [32, 96, 128, 128], P('gy', 'gx')
- multipliers: bfloat16 [32, 88, 128, 128], P('gy', 'gx')
The draws below stay inside these ranges and needn't reach their ends.
All inputs are finite; a program needn't handle non-finite values.
Results may differ from the reference program's by a relative error of at most 0.0011.
Values may be sent and summed in bfloat16 or wider, within the bound.
A program may use at most 128 MiB of HBM per device.

```python
import math
import jax
import jax.numpy as jnp
from jax import lax

BLOCK = 128
TILES = 8
REACH = 4
ROWS = 32
TILESG = 64
N_GX = 8


def coupling_fields(key):
    key_tau = jax.random.fold_in(key, 31)
    key_base = jax.random.fold_in(key, 32)
    shape = (ROWS, TILESG, BLOCK)
    tau = jax.random.uniform(key_tau, shape, jnp.float32, 1.2, 1.8)
    base = jnp.exp(jax.random.uniform(key_base, shape, jnp.float32, math.log(0.05), math.log(0.5)))
    return (tau, base)


def draw_diag_blocks(key, part):
    tau, base = coupling_fields(key)
    key_off = jax.random.fold_in(key, 12)
    shape = (ROWS, TILESG, BLOCK, BLOCK)
    spread = 0.02 * jnp.clip(jax.random.normal(key_off, shape, jnp.float32), -6.0, 6.0)
    middle = base + jnp.roll(tau, 1, axis=1) + tau
    eye = jnp.eye(BLOCK, dtype=jnp.float32)
    blocks = spread * (1.0 - eye) + middle[..., None] * eye
    return blocks.astype(jnp.bfloat16)


def draw_edge_blocks(key, part):
    tau, base = coupling_fields(key)
    key_off = jax.random.fold_in(key, 13)
    shape = (ROWS, TILESG, 2, BLOCK, BLOCK)
    spread = 0.02 * jnp.clip(jax.random.normal(key_off, shape, jnp.float32), -6.0, 6.0)
    eye = jnp.eye(BLOCK, dtype=jnp.float32)
    blocks = spread * (1.0 - eye) - tau[:, :, None, :, None] * eye
    return blocks.astype(jnp.bfloat16)


def plant(values, own_key, smallest, top_value):
    spot = [jax.random.randint(jax.random.fold_in(own_key, axis), (), 0, length) for axis, length in enumerate(values.shape)]
    widest = values.shape.index(max(values.shape))
    next_to = spot[:widest] + [(spot[widest] + 1) % values.shape[widest]] + spot[widest + 1:]
    return values.at[tuple(spot)].set(smallest).at[tuple(next_to)].set(top_value)


def setup_inputs(seed: int = 0) -> dict:
    key_list = jax.random.split(jax.random.key(seed), 5)
    return {
        "diag_blocks": draw_diag_blocks(jax.random.fold_in(key_list[4], 71), 0),
        "edge_blocks": draw_edge_blocks(jax.random.fold_in(key_list[4], 71), 0),
        "left_pick": plant(jax.random.randint(key_list[2], (ROWS, N_GX), 0 - REACH, REACH + 1), jax.random.fold_in(key_list[2], 1), 0 - REACH, REACH).astype(jnp.int32),
        "right_pick": plant(jax.random.randint(key_list[3], (ROWS, N_GX), 0 - REACH, REACH + 1), jax.random.fold_in(key_list[3], 1), 0 - REACH, REACH).astype(jnp.int32),
    }


def newton(schur):
    size = schur.shape[-1]
    eye = jnp.eye(size, dtype=schur.dtype)
    inverse_diag = 1.0 / jnp.diagonal(schur, axis1=-2, axis2=-1)
    first = 2.0 * eye * inverse_diag[..., None, :] - inverse_diag[..., :, None] * schur * inverse_diag[..., None, :]
    inner = jnp.einsum("bij,bjk->bik", schur, first, precision=lax.Precision.HIGHEST)
    return 2.0 * first - jnp.einsum("bij,bjk->bik", first, inner, precision=lax.Precision.HIGHEST)


def factor(band_diag, upper, lower):
    start = newton(band_diag[:, 0])

    def advance(previous, items):
        block, up_link, low_link = items
        mult = jnp.einsum("bij,bjk->bik", low_link, previous, precision=lax.Precision.HIGHEST)
        schur = block - jnp.einsum("bij,bjk->bik", mult, up_link, precision=lax.Precision.HIGHEST)
        pivot = newton(schur)
        return pivot, (pivot, mult)

    items = (jnp.moveaxis(band_diag[:, 1:], 1, 0), jnp.moveaxis(upper, 1, 0), jnp.moveaxis(lower, 1, 0))
    _, (later, mults) = lax.scan(advance, start, items)
    pivots = jnp.concatenate([start[:, None], jnp.moveaxis(later, 0, 1)], axis=1)
    return pivots.astype(jnp.bfloat16), jnp.moveaxis(mults, 0, 1).astype(jnp.bfloat16)


def reference(diag_blocks, edge_blocks, left_pick, right_pick):
    lines = jnp.arange(ROWS, dtype=jnp.int32)
    pivot_cols = []
    mult_cols = []
    for column in range(N_GX):
        before = (column - 1) % N_GX
        after = (column + 1) % N_GX
        left_rows = jnp.clip(lines + left_pick[:, column], 0, ROWS - 1).astype(jnp.int32)
        right_rows = jnp.clip(lines + right_pick[:, column], 0, ROWS - 1).astype(jnp.int32)
        low_end = before * TILES + TILES - 2
        left_diag = diag_blocks[:, low_end:low_end + 2][left_rows]
        left_edge = edge_blocks[:, low_end:low_end + 2][left_rows]
        right_diag = diag_blocks[:, after * TILES:after * TILES + 2][right_rows]
        right_edge = edge_blocks[:, after * TILES:after * TILES + 1][right_rows]
        own_diag = diag_blocks[:, column * TILES:(column + 1) * TILES]
        own_edge = edge_blocks[:, column * TILES:(column + 1) * TILES]
        band_diag = jnp.concatenate([left_diag, own_diag, right_diag], axis=1).astype(jnp.float32)
        links = jnp.concatenate([left_edge, own_edge, right_edge], axis=1).astype(jnp.float32)
        pivots, mults = factor(band_diag, links[:, :, 0], links[:, :, 1])
        pivot_cols.append(pivots)
        mult_cols.append(mults)
    return jnp.concatenate(pivot_cols, axis=1), jnp.concatenate(mult_cols, axis=1)
```

```python
import functools

import jax
import jax.numpy as jnp
from jax import lax
from jax.experimental import pallas as pl
from jax.experimental.pallas import tpu as pltpu
from jax.sharding import PartitionSpec as P

REACH = 4
F32 = jnp.float32
BF16 = jnp.bfloat16


def dot(a, b):
    return lax.dot_general(a, b, (((1,), (0,)), ((), ())), preferred_element_type=F32)


def split(x):
    high = x.astype(BF16)
    return high, (x - high.astype(F32)).astype(BF16)


def wide(*parts):
    return jnp.concatenate(parts, axis=1)


def tall(*parts):
    return jnp.concatenate(parts, axis=0)


def newton_all(schurs):
    size = schurs[0].shape[-1]
    rows = lax.broadcasted_iota(jnp.int32, (size, size), 0)
    cols = lax.broadcasted_iota(jnp.int32, (size, size), 1)
    on = rows == cols
    state = []
    for s in schurs:
        d_row = 1.0 / jnp.sum(jnp.where(on, s, 0.0), axis=0, keepdims=True)
        r = jnp.where(on, 0.0, s) * d_row
        rh, rl = split(r)
        state.append((d_row, r, rh, rl))
    squares = [dot(wide(rh, rl), tall(rh, rh)) + dot(rh, rl) for _, _, rh, rl in state]
    out = []
    for (d_row, r, rh, rl), r2 in zip(state, squares):
        sh, sl = split(r2)
        r3 = dot(wide(rh, rl), tall(sh, sh)) + dot(rh, sl)
        d_col = jnp.sum(jnp.where(on, d_row, 0.0), axis=1, keepdims=True)
        out.append(d_col * (jnp.where(on, 1.0, 0.0) - r + r2 - r3))
    return out


def times_link(low, stacked):
    return dot(wide(low, low), stacked)


def times_exact(m, up):
    mh, ml = split(m)
    return dot(wide(mh, ml), tall(up, up))


def stack_split(p):
    return tall(*split(p))


def rim_kernel(diag, edge, c_a, c_b, out_a, out_b):
    lines = diag.shape[0]
    half = lines // 2
    group = range(lines)

    def put(i, slot, value):
        if i < half:
            out_a[i, slot] = value.astype(BF16)
        else:
            out_b[i - half, slot] = value.astype(BF16)

    p = newton_all([diag[i, 0].astype(F32) for i in group])
    for i in group:
        put(i, 0, p[i])
    m = [times_link(edge[i, 0, 1], stack_split(p[i])) for i in group]
    for i in group:
        put(i, 2, m[i])
    s = [diag[i, 1].astype(F32) - times_exact(m[i], edge[i, 0, 0]) for i in group]
    p = newton_all(s)
    for i in group:
        put(i, 1, p[i])
    m = [times_link(edge[i, 1, 1], stack_split(p[i])) for i in group]
    for i in group:
        put(i, 3, m[i])
        c = times_exact(m[i], edge[i, 1, 0])
        if i < half:
            c_a[i] = c
        else:
            c_b[i - half] = c


def pick(at, i, lines, own_a, own_b, prev, nxt):
    half = lines // 2
    j = at[i]
    in_a = own_a[jnp.clip(j, 0, half - 1)]
    in_b = own_b[jnp.clip(j - half, 0, half - 1)]
    value = jnp.where(j < half, in_a, in_b)
    if i < half:
        return jnp.where(j < 0, prev[jnp.clip(j + half, 0, half - 1)], value)
    return jnp.where(j >= lines, nxt[jnp.clip(j - lines, 0, half - 1)], value)


def advance(blocks, ups, lows, stacked):
    group = range(len(blocks))
    m = [times_link(lows[i], stacked[i]) for i in group]
    s = [blocks[i].astype(F32) - times_exact(m[i], ups[i]) for i in group]
    return m, newton_all(s)


def chain_kernel(at, diag, edge, c_a, c_b, c_prev, c_next, piv, mul, last, carry):
    lines = diag.shape[0]
    group = range(lines)
    k = pl.program_id(0)

    def keep(p):
        for i in group:
            piv[i, 0] = p[i].astype(BF16)
            carry[i] = stack_split(p[i])

    @pl.when(k == 0)
    def _():
        s = [
            diag[i, 0].astype(F32) - pick(at, i, lines, c_a, c_b, c_prev, c_next)
            for i in group
        ]
        keep(newton_all(s))

    @pl.when(k > 0)
    def _():
        m, p = advance(
            [diag[i, 0] for i in group],
            [edge[i, 0, 0] for i in group],
            [edge[i, 0, 1] for i in group],
            [carry[i] for i in group],
        )
        for i in group:
            mul[i, 0] = m[i].astype(BF16)
        keep(p)

    @pl.when(k == pl.num_programs(0) - 1)
    def _():
        last[...] = carry[...]


def tail_kernel(at, edge, last, own_a, own_b, prev, nxt, piv_in, mul_in, piv, mul, carry):
    lines = edge.shape[0]
    group = range(lines)
    k = pl.program_id(0)

    def rim(slot, i):
        return pick(at, i, lines, *(ref.at[:, slot] for ref in (own_a, own_b, prev, nxt)))

    def keep(m, p):
        for i in group:
            mul[i, 0] = m[i].astype(BF16)
            piv[i, 0] = p[i].astype(BF16)

    @pl.when(k == 0)
    def _():
        m, p = advance(
            [rim(0, i) for i in group],
            [edge[i, 0, 0] for i in group],
            [edge[i, 0, 1] for i in group],
            [last[i] for i in group],
        )
        keep(m, p)
        for i in group:
            carry[i] = stack_split(p[i])

    @pl.when(k == 1)
    def _():
        m, p = advance(
            [rim(1, i) for i in group],
            [rim(2, i) for i in group],
            [rim(3, i) for i in group],
            [carry[i] for i in group],
        )
        keep(m, p)


def place_kernel(at, own_a, own_b, prev, nxt, piv_in, mul_in, piv, mul):
    lines = piv.shape[0]
    for i in range(lines):
        for slot in range(2):
            piv[i, slot] = pick(at, i, lines, *(r.at[:, slot] for r in (own_a, own_b, prev, nxt)))
            mul[i, slot] = pick(at, i, lines, *(r.at[:, 2 + slot] for r in (own_a, own_b, prev, nxt)))


SMEM = pl.BlockSpec(memory_space=pltpu.SMEM)
VMEM = pl.BlockSpec(memory_space=pltpu.VMEM)
ANY = pl.BlockSpec(memory_space=pl.ANY)


def params():
    return pltpu.CompilerParams(vmem_limit_bytes=48 * 2**20)


def shape(*dims, dtype=BF16):
    return jax.ShapeDtypeStruct(dims, dtype)


def cost(products, size, moved):
    return pl.CostEstimate(
        flops=6 * products * size**3, bytes_accessed=moved * size * size * 2, transcendentals=0
    )


def exchange(low, high):
    count = lax.axis_size("gy")
    prev = lax.ppermute(high, "gy", [(i, i + 1) for i in range(count - 1)])
    nxt = lax.ppermute(low, "gy", [(i + 1, i) for i in range(count - 1)])
    return low, high, prev, nxt


def shifted(array, by):
    peers = lax.axis_size("gx")
    return lax.ppermute(array, "gx", [(i, (i + by) % peers) for i in range(peers)])


def on_device(diag_blocks, edge_blocks, left_pick, right_pick):
    lines, tiles, size, _ = diag_blocks.shape
    half = lines // 2
    tile = (size, size)

    heads = jnp.concatenate([diag_blocks[:, :2], edge_blocks[:, 0]], axis=1)
    right = exchange(shifted(heads[:half], -1), shifted(heads[half:], -1))

    end = tiles // 2 - 1
    c_a, c_b, out_a, out_b = pl.pallas_call(
        rim_kernel,
        grid=(1,),
        in_specs=[
            pl.BlockSpec((lines, 2) + tile, lambda k: (0, end, 0, 0)),
            pl.BlockSpec((lines, 2, 2) + tile, lambda k: (0, end, 0, 0, 0)),
        ],
        out_specs=[VMEM] * 4,
        out_shape=[
            shape(half, *tile, dtype=F32),
            shape(half, *tile, dtype=F32),
            shape(half, 4, *tile),
            shape(half, 4, *tile),
        ],
        compiler_params=params(),
        cost_estimate=cost(lines * 8, size, lines * 12),
        name="rim",
    )(diag_blocks, edge_blocks)
    starts = exchange(shifted(c_a, 1), shifted(c_b, 1))
    left = exchange(shifted(out_a, 1), shifted(out_b, 1))

    row_count = lines * lax.axis_size("gy")
    first_row = lax.axis_index("gy") * lines
    own_rows = first_row + jnp.arange(lines, dtype=jnp.int32)
    left_at = jnp.clip(own_rows + left_pick[:, 0], 0, row_count - 1) - first_row
    right_at = jnp.clip(own_rows + right_pick[:, 0], 0, row_count - 1) - first_row

    piv_shape = shape(lines, tiles + 4, *tile)
    mul_shape = shape(lines, tiles + 3, *tile)
    piv, mul, last = pl.pallas_call(
        chain_kernel,
        grid=(tiles,),
        in_specs=[
            SMEM,
            pl.BlockSpec((lines, 1) + tile, lambda k: (0, k, 0, 0)),
            pl.BlockSpec((lines, 1, 2) + tile, lambda k: (0, jnp.maximum(k - 1, 0), 0, 0, 0)),
            VMEM,
            VMEM,
            VMEM,
            VMEM,
        ],
        out_specs=[
            pl.BlockSpec((lines, 1) + tile, lambda k: (0, k + 2, 0, 0)),
            pl.BlockSpec((lines, 1) + tile, lambda k: (0, jnp.maximum(k, 1) + 1, 0, 0)),
            VMEM,
        ],
        out_shape=[piv_shape, mul_shape, shape(lines, 2 * size, size)],
        scratch_shapes=[pltpu.VMEM((lines, 2 * size, size), BF16)],
        compiler_params=params(),
        cost_estimate=cost(lines * tiles * 4, size, lines * tiles * 5),
        name="chain",
    )(left_at, diag_blocks, edge_blocks, *starts)

    piv, mul = pl.pallas_call(
        tail_kernel,
        grid=(2,),
        in_specs=[
            SMEM,
            pl.BlockSpec((lines, 1, 2) + tile, lambda k: (0, tiles - 1, 0, 0, 0)),
            VMEM,
            VMEM,
            VMEM,
            VMEM,
            VMEM,
            ANY,
            ANY,
        ],
        out_specs=[
            pl.BlockSpec((lines, 1) + tile, lambda k: (0, tiles + 2 + k, 0, 0)),
            pl.BlockSpec((lines, 1) + tile, lambda k: (0, tiles + 1 + k, 0, 0)),
        ],
        out_shape=[piv_shape, mul_shape],
        input_output_aliases={7: 0, 8: 1},
        scratch_shapes=[pltpu.VMEM((lines, 2 * size, size), BF16)],
        compiler_params=params(),
        cost_estimate=cost(lines * 8, size, lines * 14),
        name="tail",
    )(right_at, edge_blocks, last, *right, piv, mul)

    return pl.pallas_call(
        place_kernel,
        grid=(1,),
        in_specs=[SMEM, VMEM, VMEM, VMEM, VMEM, ANY, ANY],
        out_specs=[
            pl.BlockSpec((lines, 2) + tile, lambda k: (0, 0, 0, 0)),
            pl.BlockSpec((lines, 2) + tile, lambda k: (0, 0, 0, 0)),
        ],
        out_shape=[piv_shape, mul_shape],
        input_output_aliases={5: 0, 6: 1},
        compiler_params=params(),
        cost_estimate=cost(0, size, lines * 12),
        name="place",
    )(left_at, *left, piv, mul)


def solution(mesh):
    return jax.shard_map(
        on_device,
        mesh=mesh,
        in_specs=(
            P("gy", "gx", None, None),
            P("gy", "gx", None, None, None),
            P("gy", "gx"),
            P("gy", "gx"),
        ),
        out_specs=(P("gy", "gx", None, None), P("gy", "gx", None, None)),
        check_vma=False,
    )
```

```python
import functools

import jax
import jax.numpy as jnp
from jax import lax
from jax.experimental import pallas as pl
from jax.experimental.pallas import tpu as pltpu
from jax.sharding import PartitionSpec as P

F32 = jnp.float32
BF16 = jnp.bfloat16
MESH = pl.DeviceIdType.MESH


def dot(a, b):
    return lax.dot_general(a, b, (((1,), (0,)), ((), ())), preferred_element_type=F32)


def split(x):
    high = x.astype(BF16)
    return high, (x - high.astype(F32)).astype(BF16)


def wide(*parts):
    return jnp.concatenate(parts, axis=1)


def tall(*parts):
    return jnp.concatenate(parts, axis=0)


def newton_all(schurs):
    size = schurs[0].shape[-1]
    rows = lax.broadcasted_iota(jnp.int32, (size, size), 0)
    cols = lax.broadcasted_iota(jnp.int32, (size, size), 1)
    on = rows == cols
    state = []
    for s in schurs:
        d_row = 1.0 / jnp.sum(jnp.where(on, s, 0.0), axis=0, keepdims=True)
        r = jnp.where(on, 0.0, s) * d_row
        rh, rl = split(r)
        state.append((d_row, r, rh, rl))
    squares = [dot(wide(rh, rl), tall(rh, rh)) + dot(rh, rl) for _, _, rh, rl in state]
    out = []
    for (d_row, r, rh, rl), r2 in zip(state, squares):
        sh, sl = split(r2)
        r3 = dot(wide(rh, rl), tall(sh, sh)) + dot(rh, sl)
        d_col = jnp.sum(jnp.where(on, d_row, 0.0), axis=1, keepdims=True)
        out.append(d_col * (jnp.where(on, 1.0, 0.0) - r + r2 - r3))
    return out


def times_link(low, stacked):
    return dot(wide(low, low), stacked)


def times_exact(m, up):
    mh, ml = split(m)
    return dot(wide(mh, ml), tall(up, up))


def stack_split(p):
    return tall(*split(p))


def pick(j, i, half, own, prev, nxt):
    lines = 2 * half
    value = own[jnp.clip(j, 0, lines - 1)]
    if i < half:
        return jnp.where(j < 0, prev[jnp.clip(j + half, 0, half - 1)], value)
    return jnp.where(j >= lines, nxt[jnp.clip(j - lines, 0, half - 1)], value)


def advance(blocks, ups, lows, stacked):
    group = range(len(blocks))
    m = [times_link(lows[i], stacked[i]) for i in group]
    s = [blocks[i].astype(F32) - times_exact(m[i], ups[i]) for i in group]
    return m, newton_all(s)


def kernel(
    left_pick, right_pick, diag, edge, piv, mul,
    dv, ev, carry,
    c_out, cd_out, r_out,
    c_own, cd_own, r_own, hd_own, he_own,
    c_prev, cd_prev, r_prev, hd_prev, he_prev,
    c_next, cd_next, r_next, hd_next, he_next,
    local_sem, send_x, recv_x, send_y, recv_y,
):
    lines, tiles, size, _ = dv.shape
    half = lines // 2
    group = range(lines)
    gx, gy = lax.axis_index("gx"), lax.axis_index("gy")
    nx, ny = lax.axis_size("gx"), lax.axis_size("gy")
    ahead, behind = lax.rem(gx + 1, nx), lax.rem(gx + nx - 1, nx)
    has_prev, has_next = gy > 0, gy < ny - 1
    up, down = jnp.maximum(gy - 1, 0), jnp.minimum(gy + 1, ny - 1)
    halves = (pl.ds(0, half), pl.ds(half, half))

    def local(n, a, b):
        return pltpu.make_async_copy(a, b, local_sem.at[n])

    loads = [
        local(0, diag.at[:, pl.ds(tiles - 2, 2)], dv.at[:, pl.ds(tiles - 2, 2)]),
        local(1, edge.at[:, pl.ds(tiles - 2, 2)], ev.at[:, pl.ds(tiles - 2, 2)]),
        local(2, diag.at[:, pl.ds(0, tiles - 2)], dv.at[:, pl.ds(0, tiles - 2)]),
        local(3, edge.at[:, pl.ds(0, tiles - 2)], ev.at[:, pl.ds(0, tiles - 2)]),
    ]
    for copy in loads:
        copy.start()

    def to_x(n, a, b, x):
        return pltpu.make_async_remote_copy(
            src_ref=a, dst_ref=b, send_sem=send_x.at[n], recv_sem=recv_x.at[n],
            device_id=(x, gy), device_id_type=MESH,
        )

    def to_y(n, a, b, y):
        return pltpu.make_async_remote_copy(
            src_ref=a, dst_ref=b, send_sem=send_y.at[n], recv_sem=recv_y.at[n],
            device_id=(gx, y), device_id_type=MESH,
        )

    heads_x = [
        copy
        for h, part in enumerate(halves)
        for copy in (
            to_x(2 * h, diag.at[part, pl.ds(0, 2)], hd_own.at[part], behind),
            to_x(2 * h + 1, edge.at[part, 0], he_own.at[part], behind),
        )
    ]
    start_x = [to_x(4, cd_out, cd_own, ahead)] + [
        to_x(5 + h, c_out.at[part], c_own.at[part], ahead) for h, part in enumerate(halves)
    ]
    rims_x = [to_x(7 + h, r_out.at[part], r_own.at[part], ahead) for h, part in enumerate(halves)]

    low, high = halves
    start_y = (
        [to_y(0, cd_own.at[low], cd_next, up), to_y(1, c_own.at[low], c_next, up)],
        [to_y(2, cd_own.at[high], cd_prev, down), to_y(3, c_own.at[high], c_prev, down)],
    )
    heads_y = (
        [to_y(4, hd_own.at[low], hd_next, up), to_y(5, he_own.at[low], he_next, up)],
        [to_y(6, hd_own.at[high], hd_prev, down), to_y(7, he_own.at[high], he_prev, down)],
    )
    rims_y = ([to_y(8, r_own.at[low], r_next, up)], [to_y(9, r_own.at[high], r_prev, down)])

    def forward(copies):
        @pl.when(has_prev)
        def _():
            for copy in copies[0]:
                copy.start()

        @pl.when(has_next)
        def _():
            for copy in copies[1]:
                copy.start()

    def receive(copies):
        @pl.when(has_next)
        def _():
            for copy in copies[0]:
                copy.wait_recv()

        @pl.when(has_prev)
        def _():
            for copy in copies[1]:
                copy.wait_recv()

    def drain(copies):
        @pl.when(has_prev)
        def _():
            for copy in copies[0]:
                copy.wait_send()

        @pl.when(has_next)
        def _():
            for copy in copies[1]:
                copy.wait_send()

    barrier = pltpu.get_barrier_semaphore()
    for x in (ahead, behind):
        pl.semaphore_signal(barrier, inc=1, device_id=(x, gy), device_id_type=MESH)

    @pl.when(has_prev)
    def _():
        pl.semaphore_signal(barrier, inc=1, device_id=(gx, up), device_id_type=MESH)

    @pl.when(has_next)
    def _():
        pl.semaphore_signal(barrier, inc=1, device_id=(gx, down), device_id_type=MESH)

    pl.semaphore_wait(barrier, 2 + has_prev.astype(jnp.int32) + has_next.astype(jnp.int32))

    for copy in heads_x:
        copy.start()

    loads[0].wait()
    loads[1].wait()
    on = lax.broadcasted_iota(jnp.int32, (size, size), 0) == lax.broadcasted_iota(
        jnp.int32, (size, size), 1
    )
    t0, t1 = tiles - 2, tiles - 1
    p = newton_all([dv[i, t0].astype(F32) for i in group])
    m = [times_link(ev[i, t0, 1], stack_split(p[i])) for i in group]
    for i in group:
        r_out[i, 0] = p[i].astype(BF16)
        r_out[i, 2] = m[i].astype(BF16)
    p = newton_all([dv[i, t1].astype(F32) - times_exact(m[i], ev[i, t0, 0]) for i in group])
    m = [times_link(ev[i, t1, 1], stack_split(p[i])) for i in group]
    c = [times_exact(m[i], ev[i, t1, 0]) for i in group]
    for i in group:
        c_out[i] = c[i].astype(BF16)
        cd_out[i] = jnp.broadcast_to(
            jnp.sum(jnp.where(on, c[i], 0.0), axis=0, keepdims=True), cd_out.shape[1:]
        )
    for i in group:
        r_out[i, 1] = p[i].astype(BF16)
        r_out[i, 3] = m[i].astype(BF16)
    for copy in start_x + rims_x:
        copy.start()

    for copy in start_x:
        copy.wait_recv()
    forward(start_y)
    for copy in heads_x:
        copy.wait_recv()
    forward(heads_y)
    loads[2].wait()
    loads[3].wait()
    receive(start_y)

    first = gy * lines
    left_at = [jnp.clip(first + i + left_pick[i], 0, ny * lines - 1) - first for i in group]
    right_at = [jnp.clip(first + i + right_pick[i], 0, ny * lines - 1) - first for i in group]

    def keep(k, p):
        for i in group:
            piv[i, k] = p[i].astype(BF16)
            carry[i] = stack_split(p[i])

    def correction(i):
        off = pick(left_at[i], i, half, c_own, c_prev, c_next).astype(F32)
        main = pick(left_at[i], i, half, cd_own, cd_prev, cd_next)
        return jnp.where(on, main[0:1], off)

    keep(2, newton_all([dv[i, 0].astype(F32) - correction(i) for i in group]))

    def step(k, _):
        m, p = advance(
            [dv[i, k] for i in group],
            [ev[i, k - 1, 0] for i in group],
            [ev[i, k - 1, 1] for i in group],
            [carry[i] for i in group],
        )
        for i in group:
            mul[i, k + 1] = m[i].astype(BF16)
        keep(k + 2, p)
        return 0

    middle = tiles // 2
    lax.fori_loop(1, middle, step, 0)
    for copy in rims_x:
        copy.wait_recv()
    forward(rims_y)
    lax.fori_loop(middle, tiles, step, 0)

    receive(heads_y)

    def rim(i, slot):
        refs = (hd_own, hd_prev, hd_next) if slot < 2 else (he_own, he_prev, he_next)
        return pick(right_at[i], i, half, *(ref.at[:, slot % 2] for ref in refs))

    for k in range(2):
        m, p = advance(
            [rim(i, k) for i in group],
            [ev[i, tiles - 1, 0] if k == 0 else rim(i, 2) for i in group],
            [ev[i, tiles - 1, 1] if k == 0 else rim(i, 3) for i in group],
            [carry[i] for i in group],
        )
        for i in group:
            mul[i, tiles + 1 + k] = m[i].astype(BF16)
        keep(tiles + 2 + k, p)

    receive(rims_y)
    for i in group:
        for slot in range(4):
            value = pick(left_at[i], i, half, *(r.at[:, slot] for r in (r_own, r_prev, r_next)))
            if slot < 2:
                piv[i, slot] = value
            else:
                mul[i, slot - 2] = value

    for copy in heads_x + start_x + rims_x:
        copy.wait_send()
    for copies in (start_y, heads_y, rims_y):
        drain(copies)


def on_device(diag_blocks, edge_blocks, left_pick, right_pick):
    lines, tiles, size, _ = diag_blocks.shape
    half = lines // 2
    tile = (size, size)

    def buffers(count):
        return [
            pltpu.VMEM((count,) + tile, BF16),
            pltpu.VMEM((count, 8, size), F32),
            pltpu.VMEM((count, 4) + tile, BF16),
            pltpu.VMEM((count, 2) + tile, BF16),
            pltpu.VMEM((count, 2) + tile, BF16),
        ]

    own, out, prev, nxt = buffers(lines), buffers(lines)[:3], buffers(half), buffers(half)
    vmem = pl.BlockSpec(memory_space=pltpu.VMEM)
    smem = pl.BlockSpec(memory_space=pltpu.SMEM)
    hbm = pl.BlockSpec(memory_space=pl.ANY)
    return pl.pallas_call(
        kernel,
        in_specs=[smem, smem, hbm, hbm],
        out_specs=[vmem, vmem],
        out_shape=[
            jax.ShapeDtypeStruct((lines, tiles + 4) + tile, BF16),
            jax.ShapeDtypeStruct((lines, tiles + 3) + tile, BF16),
        ],
        scratch_shapes=[
            pltpu.VMEM((lines, tiles) + tile, BF16),
            pltpu.VMEM((lines, tiles, 2) + tile, BF16),
            pltpu.VMEM((lines, 2 * size, size), BF16),
        ]
        + out + own + prev + nxt
        + [pltpu.SemaphoreType.DMA((n,)) for n in (4, 9, 9, 10, 10)],
        compiler_params=pltpu.CompilerParams(
            collective_id=0, has_side_effects=True, vmem_limit_bytes=56 * 2**20
        ),
        name="subdomains",
    )(left_pick[:, 0], right_pick[:, 0], diag_blocks, edge_blocks)


def solution(mesh):
    return jax.shard_map(
        on_device,
        mesh=mesh,
        in_specs=(
            P("gy", "gx", None, None),
            P("gy", "gx", None, None, None),
            P("gy", "gx"),
            P("gy", "gx"),
        ),
        out_specs=(P("gy", "gx", None, None), P("gy", "gx", None, None)),
        check_vma=False,
    )
```

```python
import functools

import jax
import jax.numpy as jnp
from jax import lax
from jax.experimental import pallas as pl
from jax.experimental.pallas import tpu as pltpu
from jax.sharding import PartitionSpec as P

F32 = jnp.float32
BF16 = jnp.bfloat16
MESH = pl.DeviceIdType.MESH


def dot(a, b):
    return lax.dot_general(a, b, (((1,), (0,)), ((), ())), preferred_element_type=F32)


def split(x):
    high = x.astype(BF16)
    return high, (x - high.astype(F32)).astype(BF16)


def wide(*parts):
    return jnp.concatenate(parts, axis=1)


def tall(*parts):
    return jnp.concatenate(parts, axis=0)


def newton_all(schurs):
    size = schurs[0].shape[-1]
    rows = lax.broadcasted_iota(jnp.int32, (size, size), 0)
    cols = lax.broadcasted_iota(jnp.int32, (size, size), 1)
    on = rows == cols
    state = []
    for s in schurs:
        d_row = 1.0 / jnp.sum(jnp.where(on, s, 0.0), axis=0, keepdims=True)
        r = jnp.where(on, 0.0, s) * d_row
        rh, rl = split(r)
        state.append((d_row, r, rh, rl))
    squares = [dot(wide(rh, rl), tall(rh, rh)) + dot(rh, rl) for _, _, rh, rl in state]
    out = []
    for (d_row, r, rh, rl), r2 in zip(state, squares):
        sh, sl = split(r2)
        r3 = dot(wide(rh, rl), tall(sh, sh)) + dot(rh, sl)
        d_col = jnp.sum(jnp.where(on, d_row, 0.0), axis=1, keepdims=True)
        out.append(d_col * (jnp.where(on, 1.0, 0.0) - r + r2 - r3))
    return out


def times_link(low, stacked):
    return dot(wide(low, low), stacked)


def times_exact(m, up):
    mh, ml = split(m)
    return dot(wide(mh, ml), tall(up, up))


def stack_split(p):
    return tall(*split(p))


def pick(j, i, half, own, prev, nxt):
    lines = 2 * half
    value = own[jnp.clip(j, 0, lines - 1)]
    if i < half:
        return jnp.where(j < 0, prev[jnp.clip(j + half, 0, half - 1)], value)
    return jnp.where(j >= lines, nxt[jnp.clip(j - lines, 0, half - 1)], value)


def advance(blocks, ups, lows, stacked):
    group = range(len(blocks))
    m = [times_link(lows[i], stacked[i]) for i in group]
    s = [blocks[i].astype(F32) - times_exact(m[i], ups[i]) for i in group]
    return m, newton_all(s)


def kernel(
    left_pick, right_pick, diag, edge, piv, mul,
    dv, ev, carry,
    c_out, cd_out, r_out,
    c_own, cd_own, r_own, hd_own, he_own,
    c_prev, cd_prev, r_prev, hd_prev, he_prev,
    c_next, cd_next, r_next, hd_next, he_next,
    relay_a, relay_b,
    local_sem, send_x, recv_x, send_y, recv_y, send_r, recv_r,
):
    lines, tiles, size, _ = dv.shape
    half = lines // 2
    group = range(lines)
    gx, gy = lax.axis_index("gx"), lax.axis_index("gy")
    nx, ny = lax.axis_size("gx"), lax.axis_size("gy")
    ahead, behind = lax.rem(gx + 1, nx), lax.rem(gx + nx - 1, nx)
    has_prev, has_next = gy > 0, gy < ny - 1
    up, down = jnp.maximum(gy - 1, 0), jnp.minimum(gy + 1, ny - 1)
    halves = (pl.ds(0, half), pl.ds(half, half))

    def local(n, a, b):
        return pltpu.make_async_copy(a, b, local_sem.at[n])

    loads = [
        local(0, diag.at[:, pl.ds(tiles - 2, 2)], dv.at[:, pl.ds(tiles - 2, 2)]),
        local(1, edge.at[:, pl.ds(tiles - 2, 2)], ev.at[:, pl.ds(tiles - 2, 2)]),
        local(2, diag.at[:, pl.ds(0, tiles - 2)], dv.at[:, pl.ds(0, tiles - 2)]),
        local(3, edge.at[:, pl.ds(0, tiles - 2)], ev.at[:, pl.ds(0, tiles - 2)]),
    ]
    for copy in loads:
        copy.start()

    def to_x(n, a, b, x):
        return pltpu.make_async_remote_copy(
            src_ref=a, dst_ref=b, send_sem=send_x.at[n], recv_sem=recv_x.at[n],
            device_id=(x, gy), device_id_type=MESH,
        )

    def to_y(n, a, b, y):
        return pltpu.make_async_remote_copy(
            src_ref=a, dst_ref=b, send_sem=send_y.at[n], recv_sem=recv_y.at[n],
            device_id=(gx, y), device_id_type=MESH,
        )

    heads_x = [
        copy
        for h, part in enumerate(halves)
        for copy in (
            to_x(2 * h, diag.at[part, pl.ds(0, 2)], hd_own.at[part], behind),
            to_x(2 * h + 1, edge.at[part, 0], he_own.at[part], behind),
        )
    ]
    start_x = [to_x(4, cd_out, cd_own, ahead)] + [
        to_x(5 + h, c_out.at[part], c_own.at[part], ahead) for h, part in enumerate(halves)
    ]
    rims_x = [to_x(7 + h, r_out.at[part], r_own.at[part], ahead) for h, part in enumerate(halves)]

    low, high = halves
    start_y = (
        [to_y(0, cd_own.at[low], cd_next, up), to_y(1, c_own.at[low], c_next, up)],
        [to_y(2, cd_own.at[high], cd_prev, down), to_y(3, c_own.at[high], c_prev, down)],
    )
    heads_y = (
        [to_y(4, hd_own.at[low], hd_next, up), to_y(5, he_own.at[low], he_next, up)],
        [to_y(6, hd_own.at[high], hd_prev, down), to_y(7, he_own.at[high], he_prev, down)],
    )
    rims_y = ([to_y(8, r_own.at[low], r_next, up)], [to_y(9, r_own.at[high], r_prev, down)])

    odd = lax.rem(gy, 2) == 1
    paired = ny % 2 == 0 and ny > 2
    cross_up = jnp.logical_and(has_prev, jnp.logical_not(odd))
    cross_down = jnp.logical_and(has_next, odd)
    two_up, two_down = jnp.maximum(gy - 2, 0), jnp.minimum(gy + 2, ny - 1)
    front, back = pl.ds(0, 2), pl.ds(2, 2)

    def to_r(a, b, send, recv, y):
        return pltpu.make_async_remote_copy(
            src_ref=a, dst_ref=b, send_sem=send, recv_sem=recv,
            device_id=(gx, y), device_id_type=MESH,
        )

    heads_r = (
        [
            to_r(hd_own.at[low], relay_b.at[:, front], send_y.at[4], recv_r.at[2], down),
            to_r(he_own.at[low], relay_b.at[:, back], send_y.at[5], recv_r.at[3], down),
        ],
        [
            to_r(hd_own.at[high], relay_a.at[:, front], send_y.at[6], recv_r.at[0], two_down),
            to_r(he_own.at[high], relay_a.at[:, back], send_y.at[7], recv_r.at[1], two_down),
        ],
    )
    rims_r = (
        [to_r(r_own.at[low], relay_b, send_y.at[8], recv_r.at[2], two_up)],
        [to_r(r_own.at[high], relay_a, send_y.at[9], recv_r.at[0], up)],
    )
    heads_pass = [
        to_r(relay_a.at[:, front], hd_prev, send_r.at[0], recv_y.at[6], up),
        to_r(relay_a.at[:, back], he_prev, send_r.at[1], recv_y.at[7], up),
        to_r(relay_b.at[:, front], hd_next, send_r.at[2], recv_y.at[4], two_up),
        to_r(relay_b.at[:, back], he_next, send_r.at[3], recv_y.at[5], two_up),
    ]
    rims_pass = [
        to_r(relay_a, r_prev, send_r.at[0], recv_y.at[9], two_down),
        to_r(relay_b, r_next, send_r.at[2], recv_y.at[8], down),
    ]
    passes_heads = jnp.logical_and(odd, gy > 2)
    passes_rims = jnp.logical_and(jnp.logical_not(odd), gy + 2 < ny)

    def pass_on(incoming, outgoing, cond):
        if paired:
            @pl.when(cond)
            def _():
                for copy, onward in zip(incoming[1] + incoming[0], outgoing):
                    copy.wait_recv()
                    onward.start()

    def forward(copies, relayed=None):
        direct_up, direct_down = has_prev, has_next
        if relayed is not None and paired:
            direct_up = jnp.logical_and(has_prev, odd)
            direct_down = jnp.logical_and(has_next, jnp.logical_not(odd))

            @pl.when(cross_down)
            def _():
                for copy in relayed[1]:
                    copy.start()

            @pl.when(cross_up)
            def _():
                for copy in relayed[0]:
                    copy.start()

        @pl.when(direct_up)
        def _():
            for copy in copies[0]:
                copy.start()

        @pl.when(direct_down)
        def _():
            for copy in copies[1]:
                copy.start()

    def receive(copies):
        @pl.when(has_next)
        def _():
            for copy in copies[0]:
                copy.wait_recv()

        @pl.when(has_prev)
        def _():
            for copy in copies[1]:
                copy.wait_recv()

    def drain(copies):
        @pl.when(has_prev)
        def _():
            for copy in copies[0]:
                copy.wait_send()

        @pl.when(has_next)
        def _():
            for copy in copies[1]:
                copy.wait_send()

    barrier = pltpu.get_barrier_semaphore()
    for x in (ahead, behind):
        pl.semaphore_signal(barrier, inc=1, device_id=(x, gy), device_id_type=MESH)

    peers = 2
    for reach in (1, 2):
        for there, y in ((gy >= reach, gy - reach), (gy + reach < ny, gy + reach)):
            peers += there.astype(jnp.int32)

            @pl.when(there)
            def _():
                pl.semaphore_signal(
                    barrier, inc=1, device_id=(gx, jnp.clip(y, 0, ny - 1)), device_id_type=MESH
                )

    pl.semaphore_wait(barrier, peers)

    for copy in heads_x:
        copy.start()

    loads[0].wait()
    loads[1].wait()
    on = lax.broadcasted_iota(jnp.int32, (size, size), 0) == lax.broadcasted_iota(
        jnp.int32, (size, size), 1
    )
    t0, t1 = tiles - 2, tiles - 1
    p = newton_all([dv[i, t0].astype(F32) for i in group])
    m = [times_link(ev[i, t0, 1], stack_split(p[i])) for i in group]
    for i in group:
        r_out[i, 0] = p[i].astype(BF16)
        r_out[i, 2] = m[i].astype(BF16)
    p = newton_all([dv[i, t1].astype(F32) - times_exact(m[i], ev[i, t0, 0]) for i in group])
    m = [times_link(ev[i, t1, 1], stack_split(p[i])) for i in group]
    c = [times_exact(m[i], ev[i, t1, 0]) for i in group]
    for i in group:
        c_out[i] = c[i].astype(BF16)
        cd_out[i] = jnp.broadcast_to(
            jnp.sum(jnp.where(on, c[i], 0.0), axis=0, keepdims=True), cd_out.shape[1:]
        )
    for i in group:
        r_out[i, 1] = p[i].astype(BF16)
        r_out[i, 3] = m[i].astype(BF16)
    for copy in start_x + rims_x:
        copy.start()

    for copy in start_x:
        copy.wait_recv()
    forward(start_y)
    for copy in heads_x:
        copy.wait_recv()
    forward(heads_y, heads_r)
    loads[2].wait()
    loads[3].wait()
    receive(start_y)

    first = gy * lines
    left_at = [jnp.clip(first + i + left_pick[i], 0, ny * lines - 1) - first for i in group]
    right_at = [jnp.clip(first + i + right_pick[i], 0, ny * lines - 1) - first for i in group]

    def keep(k, p):
        for i in group:
            piv[i, k] = p[i].astype(BF16)
            carry[i] = stack_split(p[i])

    def correction(i):
        off = pick(left_at[i], i, half, c_own, c_prev, c_next).astype(F32)
        main = pick(left_at[i], i, half, cd_own, cd_prev, cd_next)
        return jnp.where(on, main[0:1], off)

    keep(2, newton_all([dv[i, 0].astype(F32) - correction(i) for i in group]))

    def step(k, _):
        m, p = advance(
            [dv[i, k] for i in group],
            [ev[i, k - 1, 0] for i in group],
            [ev[i, k - 1, 1] for i in group],
            [carry[i] for i in group],
        )
        for i in group:
            mul[i, k + 1] = m[i].astype(BF16)
        keep(k + 2, p)
        return 0

    middle = tiles // 2
    lax.fori_loop(1, middle, step, 0)
    pass_on(heads_r, heads_pass, passes_heads)
    for copy in rims_x:
        copy.wait_recv()
    forward(rims_y, rims_r)
    lax.fori_loop(middle, tiles, step, 0)

    receive(heads_y)

    def rim(i, slot):
        refs = (hd_own, hd_prev, hd_next) if slot < 2 else (he_own, he_prev, he_next)
        return pick(right_at[i], i, half, *(ref.at[:, slot % 2] for ref in refs))

    for k in range(2):
        m, p = advance(
            [rim(i, k) for i in group],
            [ev[i, tiles - 1, 0] if k == 0 else rim(i, 2) for i in group],
            [ev[i, tiles - 1, 1] if k == 0 else rim(i, 3) for i in group],
            [carry[i] for i in group],
        )
        for i in group:
            mul[i, tiles + 1 + k] = m[i].astype(BF16)
        keep(tiles + 2 + k, p)

    pass_on(rims_r, rims_pass, passes_rims)
    receive(rims_y)
    for i in group:
        for slot in range(4):
            value = pick(left_at[i], i, half, *(r.at[:, slot] for r in (r_own, r_prev, r_next)))
            if slot < 2:
                piv[i, slot] = value
            else:
                mul[i, slot - 2] = value

    for copy in heads_x + start_x + rims_x:
        copy.wait_send()
    for copies in (start_y, heads_y, rims_y):
        drain(copies)
    if paired:
        for cond, copies in ((passes_heads, heads_pass), (passes_rims, rims_pass)):

            @pl.when(cond)
            def _():
                for copy in copies:
                    copy.wait_send()


def on_device(diag_blocks, edge_blocks, left_pick, right_pick):
    lines, tiles, size, _ = diag_blocks.shape
    half = lines // 2
    tile = (size, size)

    def buffers(count):
        return [
            pltpu.VMEM((count,) + tile, BF16),
            pltpu.VMEM((count, 8, size), F32),
            pltpu.VMEM((count, 4) + tile, BF16),
            pltpu.VMEM((count, 2) + tile, BF16),
            pltpu.VMEM((count, 2) + tile, BF16),
        ]

    own, out, prev, nxt = buffers(lines), buffers(lines)[:3], buffers(half), buffers(half)
    vmem = pl.BlockSpec(memory_space=pltpu.VMEM)
    smem = pl.BlockSpec(memory_space=pltpu.SMEM)
    hbm = pl.BlockSpec(memory_space=pl.ANY)
    return pl.pallas_call(
        kernel,
        in_specs=[smem, smem, hbm, hbm],
        out_specs=[vmem, vmem],
        out_shape=[
            jax.ShapeDtypeStruct((lines, tiles + 4) + tile, BF16),
            jax.ShapeDtypeStruct((lines, tiles + 3) + tile, BF16),
        ],
        scratch_shapes=[
            pltpu.VMEM((lines, tiles) + tile, BF16),
            pltpu.VMEM((lines, tiles, 2) + tile, BF16),
            pltpu.VMEM((lines, 2 * size, size), BF16),
        ]
        + out + own + prev + nxt
        + [pltpu.VMEM((half, 4) + tile, BF16)] * 2
        + [pltpu.SemaphoreType.DMA((n,)) for n in (4, 9, 9, 10, 10, 4, 4)],
        compiler_params=pltpu.CompilerParams(
            collective_id=0, has_side_effects=True, vmem_limit_bytes=30 * 2**20
        ),
        name="subdomains",
    )(left_pick[:, 0], right_pick[:, 0], diag_blocks, edge_blocks)


def solution(mesh):
    return jax.shard_map(
        on_device,
        mesh=mesh,
        in_specs=(
            P("gy", "gx", None, None),
            P("gy", "gx", None, None, None),
            P("gy", "gx"),
            P("gy", "gx"),
        ),
        out_specs=(P("gy", "gx", None, None), P("gy", "gx", None, None)),
        check_vma=False,
    )
```

```python
import functools

import jax
import jax.numpy as jnp
from jax import lax
from jax.experimental import pallas as pl
from jax.experimental.pallas import tpu as pltpu
from jax.sharding import PartitionSpec as P

F32 = jnp.float32
BF16 = jnp.bfloat16
MESH = pl.DeviceIdType.MESH


def dot(a, b):
    return lax.dot_general(a, b, (((1,), (0,)), ((), ())), preferred_element_type=F32)


def split(x):
    high = x.astype(BF16)
    return high, (x - high.astype(F32)).astype(BF16)


def wide(*parts):
    return jnp.concatenate(parts, axis=1)


def tall(*parts):
    return jnp.concatenate(parts, axis=0)


def newton_all(schurs):
    size = schurs[0].shape[-1]
    rows = lax.broadcasted_iota(jnp.int32, (size, size), 0)
    cols = lax.broadcasted_iota(jnp.int32, (size, size), 1)
    on = rows == cols
    state = []
    for s in schurs:
        d_row = 1.0 / jnp.sum(jnp.where(on, s, 0.0), axis=0, keepdims=True)
        r = jnp.where(on, 0.0, s) * d_row
        rh, rl = split(r)
        state.append((d_row, r, rh, rl))
    squares = [dot(wide(rh, rl), tall(rh, rh)) + dot(rh, rl) for _, _, rh, rl in state]
    out = []
    for (d_row, r, rh, rl), r2 in zip(state, squares):
        sh, sl = split(r2)
        r3 = dot(wide(rh, rl), tall(sh, sh)) + dot(rh, sl)
        d_col = jnp.sum(jnp.where(on, d_row, 0.0), axis=1, keepdims=True)
        out.append(d_col * (jnp.where(on, 1.0, 0.0) - r + r2 - r3))
    return out


def times_link(low, stacked):
    return dot(wide(low, low), stacked)


def times_exact(m, up):
    mh, ml = split(m)
    return dot(wide(mh, ml), tall(up, up))


def stack_split(p):
    return tall(*split(p))


def pick(j, i, half, own, prev, nxt):
    lines = 2 * half
    value = own[jnp.clip(j, 0, lines - 1)]
    if i < half:
        return jnp.where(j < 0, prev[jnp.clip(j + half, 0, half - 1)], value)
    return jnp.where(j >= lines, nxt[jnp.clip(j - lines, 0, half - 1)], value)


def advance(blocks, ups, lows, stacked):
    group = range(len(blocks))
    m = [times_link(lows[i], stacked[i]) for i in group]
    s = [blocks[i].astype(F32) - times_exact(m[i], ups[i]) for i in group]
    return m, newton_all(s)


def kernel(
    left_pick, right_pick, diag, edge, piv, mul,
    dv, ev, carry,
    c_out, cd_out, r_out,
    c_own, cd_own, r_own, hd_own, he_own,
    c_prev, cd_prev, r_prev, hd_prev, he_prev,
    c_next, cd_next, r_next, hd_next, he_next,
    relay_a, relay_b,
    local_sem, send_x, recv_x, send_y, recv_y, send_r, recv_r,
):
    lines, tiles, size, _ = dv.shape
    half = lines // 2
    group = range(lines)
    gx, gy = lax.axis_index("gx"), lax.axis_index("gy")
    nx, ny = lax.axis_size("gx"), lax.axis_size("gy")
    ahead, behind = lax.rem(gx + 1, nx), lax.rem(gx + nx - 1, nx)
    has_prev, has_next = gy > 0, gy < ny - 1
    up, down = jnp.maximum(gy - 1, 0), jnp.minimum(gy + 1, ny - 1)
    halves = (pl.ds(0, half), pl.ds(half, half))

    def local(n, a, b):
        return pltpu.make_async_copy(a, b, local_sem.at[n])

    loads = [
        local(0, diag.at[:, pl.ds(tiles - 2, 2)], dv.at[:, pl.ds(tiles - 2, 2)]),
        local(1, edge.at[:, pl.ds(tiles - 2, 2)], ev.at[:, pl.ds(tiles - 2, 2)]),
        local(2, diag.at[:, pl.ds(0, tiles - 2)], dv.at[:, pl.ds(0, tiles - 2)]),
        local(3, edge.at[:, pl.ds(0, tiles - 2)], ev.at[:, pl.ds(0, tiles - 2)]),
    ]
    for copy in loads:
        copy.start()

    def to_x(n, a, b, x):
        return pltpu.make_async_remote_copy(
            src_ref=a, dst_ref=b, send_sem=send_x.at[n], recv_sem=recv_x.at[n],
            device_id=(x, gy), device_id_type=MESH,
        )

    def to_y(n, a, b, y):
        return pltpu.make_async_remote_copy(
            src_ref=a, dst_ref=b, send_sem=send_y.at[n], recv_sem=recv_y.at[n],
            device_id=(gx, y), device_id_type=MESH,
        )

    heads_x = [
        copy
        for h, part in enumerate(halves)
        for copy in (
            to_x(2 * h, diag.at[part, pl.ds(0, 2)], hd_own.at[part], behind),
            to_x(2 * h + 1, edge.at[part, 0], he_own.at[part], behind),
        )
    ]
    start_x = [to_x(4, cd_out, cd_own, ahead)] + [
        to_x(5 + h, c_out.at[part], c_own.at[part], ahead) for h, part in enumerate(halves)
    ]
    rims_x = [to_x(7 + h, r_out.at[part], r_own.at[part], ahead) for h, part in enumerate(halves)]

    low, high = halves
    start_y = (
        [to_y(0, cd_own.at[low], cd_next, up), to_y(1, c_own.at[low], c_next, up)],
        [to_y(2, cd_own.at[high], cd_prev, down), to_y(3, c_own.at[high], c_prev, down)],
    )
    heads_y = (
        [to_y(4, hd_own.at[low], hd_next, up), to_y(5, he_own.at[low], he_next, up)],
        [to_y(6, hd_own.at[high], hd_prev, down), to_y(7, he_own.at[high], he_prev, down)],
    )
    rims_y = ([to_y(8, r_own.at[low], r_next, up)], [to_y(9, r_own.at[high], r_prev, down)])

    odd = lax.rem(gy, 2) == 1
    paired = ny % 2 == 0 and ny > 2
    cross_up = jnp.logical_and(has_prev, jnp.logical_not(odd))
    cross_down = jnp.logical_and(has_next, odd)
    two_up, two_down = jnp.maximum(gy - 2, 0), jnp.minimum(gy + 2, ny - 1)
    front, back = pl.ds(0, 2), pl.ds(2, 2)

    def to_r(a, b, send, recv, y):
        return pltpu.make_async_remote_copy(
            src_ref=a, dst_ref=b, send_sem=send, recv_sem=recv,
            device_id=(gx, y), device_id_type=MESH,
        )

    heads_r = (
        [
            to_r(hd_own.at[low], relay_b.at[:, front], send_y.at[4], recv_r.at[2], down),
            to_r(he_own.at[low], relay_b.at[:, back], send_y.at[5], recv_r.at[3], down),
        ],
        [
            to_r(hd_own.at[high], relay_a.at[:, front], send_y.at[6], recv_r.at[0], two_down),
            to_r(he_own.at[high], relay_a.at[:, back], send_y.at[7], recv_r.at[1], two_down),
        ],
    )
    rims_r = (
        [to_r(r_own.at[low], relay_b, send_y.at[8], recv_r.at[2], two_up)],
        [to_r(r_own.at[high], relay_a, send_y.at[9], recv_r.at[0], up)],
    )
    heads_pass = [
        to_r(relay_a.at[:, front], hd_prev, send_r.at[0], recv_y.at[6], up),
        to_r(relay_a.at[:, back], he_prev, send_r.at[1], recv_y.at[7], up),
        to_r(relay_b.at[:, front], hd_next, send_r.at[2], recv_y.at[4], two_up),
        to_r(relay_b.at[:, back], he_next, send_r.at[3], recv_y.at[5], two_up),
    ]
    rims_pass = [
        to_r(relay_a, r_prev, send_r.at[0], recv_y.at[9], two_down),
        to_r(relay_b, r_next, send_r.at[2], recv_y.at[8], down),
    ]
    passes_heads = jnp.logical_and(odd, gy > 2)
    passes_rims = jnp.logical_and(jnp.logical_not(odd), gy + 2 < ny)

    def pass_on(incoming, outgoing, cond):
        if paired:
            @pl.when(cond)
            def _():
                for copy, onward in zip(incoming[1] + incoming[0], outgoing):
                    copy.wait_recv()
                    onward.start()

    def forward(copies, relayed=None):
        direct_up, direct_down = has_prev, has_next
        if relayed is not None and paired:
            direct_up = jnp.logical_and(has_prev, odd)
            direct_down = jnp.logical_and(has_next, jnp.logical_not(odd))

            @pl.when(cross_down)
            def _():
                for copy in relayed[1]:
                    copy.start()

            @pl.when(cross_up)
            def _():
                for copy in relayed[0]:
                    copy.start()

        @pl.when(direct_up)
        def _():
            for copy in copies[0]:
                copy.start()

        @pl.when(direct_down)
        def _():
            for copy in copies[1]:
                copy.start()

    def receive(copies):
        @pl.when(has_next)
        def _():
            for copy in copies[0]:
                copy.wait_recv()

        @pl.when(has_prev)
        def _():
            for copy in copies[1]:
                copy.wait_recv()

    def drain(copies):
        @pl.when(has_prev)
        def _():
            for copy in copies[0]:
                copy.wait_send()

        @pl.when(has_next)
        def _():
            for copy in copies[1]:
                copy.wait_send()

    barrier = pltpu.get_barrier_semaphore()
    for x in (ahead, behind):
        pl.semaphore_signal(barrier, inc=1, device_id=(x, gy), device_id_type=MESH)

    peers = 2
    for reach in (1, 2):
        for there, y in ((gy >= reach, gy - reach), (gy + reach < ny, gy + reach)):
            peers += there.astype(jnp.int32)

            @pl.when(there)
            def _():
                pl.semaphore_signal(
                    barrier, inc=1, device_id=(gx, jnp.clip(y, 0, ny - 1)), device_id_type=MESH
                )

    pl.semaphore_wait(barrier, peers)

    for copy in heads_x:
        copy.start()

    loads[0].wait()
    loads[1].wait()
    on = lax.broadcasted_iota(jnp.int32, (size, size), 0) == lax.broadcasted_iota(
        jnp.int32, (size, size), 1
    )
    t0, t1 = tiles - 2, tiles - 1
    p = newton_all([dv[i, t0].astype(F32) for i in group])
    m = [times_link(ev[i, t0, 1], stack_split(p[i])) for i in group]
    for i in group:
        r_out[i, 0] = p[i].astype(BF16)
        r_out[i, 2] = m[i].astype(BF16)
    p = newton_all([dv[i, t1].astype(F32) - times_exact(m[i], ev[i, t0, 0]) for i in group])
    m = [times_link(ev[i, t1, 1], stack_split(p[i])) for i in group]
    c = [times_exact(m[i], ev[i, t1, 0]) for i in group]
    for i in group:
        c_out[i] = c[i].astype(BF16)
        cd_out[i] = jnp.broadcast_to(
            jnp.sum(jnp.where(on, c[i], 0.0), axis=0, keepdims=True), cd_out.shape[1:]
        )
    for i in group:
        r_out[i, 1] = p[i].astype(BF16)
        r_out[i, 3] = m[i].astype(BF16)
    for copy in start_x + rims_x:
        copy.start()

    for copy in start_x:
        copy.wait_recv()
    forward(start_y)
    for copy in heads_x:
        copy.wait_recv()
    forward(heads_y, heads_r)
    loads[2].wait()
    loads[3].wait()
    receive(start_y)

    first = gy * lines
    left_at = [jnp.clip(first + i + left_pick[i], 0, ny * lines - 1) - first for i in group]
    right_at = [jnp.clip(first + i + right_pick[i], 0, ny * lines - 1) - first for i in group]

    def keep(k, p):
        for i in group:
            piv[i, k] = p[i].astype(BF16)
            carry[i] = stack_split(p[i])

    def correction(i):
        off = pick(left_at[i], i, half, c_own, c_prev, c_next).astype(F32)
        main = pick(left_at[i], i, half, cd_own, cd_prev, cd_next)
        return jnp.where(on, main[0:1], off)

    keep(2, newton_all([dv[i, 0].astype(F32) - correction(i) for i in group]))

    def step(k, _):
        m, p = advance(
            [dv[i, k] for i in group],
            [ev[i, k - 1, 0] for i in group],
            [ev[i, k - 1, 1] for i in group],
            [carry[i] for i in group],
        )
        for i in group:
            mul[i, k + 1] = m[i].astype(BF16)
        keep(k + 2, p)
        return 0

    middle = tiles // 2
    lax.fori_loop(1, middle, step, 0)
    pass_on(heads_r, heads_pass, passes_heads)
    for copy in rims_x:
        copy.wait_recv()
    forward(rims_y, rims_r)
    lax.fori_loop(middle, tiles, step, 0)

    receive(heads_y)

    def rim(i, slot):
        refs = (hd_own, hd_prev, hd_next) if slot < 2 else (he_own, he_prev, he_next)
        return pick(right_at[i], i, half, *(ref.at[:, slot % 2] for ref in refs))

    for k in range(2):
        m, p = advance(
            [rim(i, k) for i in group],
            [ev[i, tiles - 1, 0] if k == 0 else rim(i, 2) for i in group],
            [ev[i, tiles - 1, 1] if k == 0 else rim(i, 3) for i in group],
            [carry[i] for i in group],
        )
        for i in group:
            mul[i, tiles + 1 + k] = m[i].astype(BF16)
        keep(tiles + 2 + k, p)

    pass_on(rims_r, rims_pass, passes_rims)
    receive(rims_y)
    for i in group:
        for slot in range(4):
            value = pick(left_at[i], i, half, *(r.at[:, slot] for r in (r_own, r_prev, r_next)))
            if slot < 2:
                piv[i, slot] = value
            else:
                mul[i, slot - 2] = value

    for copy in heads_x + start_x + rims_x:
        copy.wait_send()
    for copies in (start_y, heads_y, rims_y):
        drain(copies)
    if paired:
        for cond, copies in ((passes_heads, heads_pass), (passes_rims, rims_pass)):

            @pl.when(cond)
            def _():
                for copy in copies:
                    copy.wait_send()


def on_device(diag_blocks, edge_blocks, left_pick, right_pick):
    lines, tiles, size, _ = diag_blocks.shape
    half = lines // 2
    tile = (size, size)

    def buffers(count):
        return [
            pltpu.VMEM((count,) + tile, BF16),
            pltpu.VMEM((count, 8, size), F32),
            pltpu.VMEM((count, 4) + tile, BF16),
            pltpu.VMEM((count, 2) + tile, BF16),
            pltpu.VMEM((count, 2) + tile, BF16),
        ]

    own, out, prev, nxt = buffers(lines), buffers(lines)[:3], buffers(half), buffers(half)
    vmem = pl.BlockSpec(memory_space=pltpu.VMEM)
    smem = pl.BlockSpec(memory_space=pltpu.SMEM)
    hbm = pl.BlockSpec(memory_space=pltpu.HBM)
    return pl.pallas_call(
        kernel,
        in_specs=[smem, smem, hbm, hbm],
        out_specs=[vmem, vmem],
        out_shape=[
            jax.ShapeDtypeStruct((lines, tiles + 4) + tile, BF16),
            jax.ShapeDtypeStruct((lines, tiles + 3) + tile, BF16),
        ],
        scratch_shapes=[
            pltpu.VMEM((lines, tiles) + tile, BF16),
            pltpu.VMEM((lines, tiles, 2) + tile, BF16),
            pltpu.VMEM((lines, 2 * size, size), BF16),
        ]
        + out + own + prev + nxt
        + [pltpu.VMEM((half, 4) + tile, BF16)] * 2
        + [pltpu.SemaphoreType.DMA((n,)) for n in (4, 9, 9, 10, 10, 4, 4)],
        compiler_params=pltpu.CompilerParams(
            collective_id=0, has_side_effects=True, vmem_limit_bytes=46 * 2**20
        ),
        name="subdomains",
    )(left_pick[:, 0], right_pick[:, 0], diag_blocks, edge_blocks)


def solution(mesh):
    return jax.shard_map(
        on_device,
        mesh=mesh,
        in_specs=(
            P("gy", "gx", None, None),
            P("gy", "gx", None, None, None),
            P("gy", "gx"),
            P("gy", "gx"),
        ),
        out_specs=(P("gy", "gx", None, None), P("gy", "gx", None, None)),
        check_vma=False,
    )
```
